32 devices in a mesh: row: 4 (over y, core), col: 8 (over z, x).
Axes of the slice: x: 2, y: 2, z: 4, core: 2. Of those that a mesh axis runs over, the one named last changes fastest.
Arguments:
- acts: bfloat16 [192, 2, 28672], P('col', None, 'row'), may hold values from -6 to 6
- grads: bfloat16 [192, 2, 8192], P('row', None, 'col'), may hold values from -0.3984375 to 0.3984375
- basis_in: bfloat16 [28672, 28672], P('row', 'col'), may hold values from -0.03125 to 0.03125
- basis_out: bfloat16 [8192, 8192], P('col', 'row'), may hold values from -0.0625 to 0.0625
- eigen: bfloat16 [28672, 8192], P('col', 'row'), may hold values from 0.5 to 8
- sketch: bfloat16 [72, 8192], P(None, 'col'), may hold values from -0.0625 to 0.0625
Outputs:
- range_basis: float32 [2, 72, 28672], P(None, None, 'row')
- projected: float32 [2, 72, 8192], P(None, None, 'col')
The draws below stay inside these ranges and needn't reach their ends.
All inputs are finite; a program needn't handle non-finite values.
Results may differ from the reference program's by a relative error of at most 0.018.
Values may be sent and summed in bfloat16 or wider, within the bound.
A program may use at most 192 MiB of HBM per device.

```python
import math
import jax
import jax.numpy as jnp
from jax import lax

IN = 28672
OUT = 8192
SK = 72
NQ = 2
TOK = 192


def steps_of(own_key, shape, shards, low, largest):
    loudness = 1.0
    for position, parts in shards:
        steps = jax.random.uniform(jax.random.fold_in(jax.random.fold_in(own_key, 6), position), (parts,), jnp.float32, low / len(shards), largest / len(shards))
        loudness = loudness * jnp.repeat(jnp.exp(steps), shape[position] // parts).reshape((-1,) + (1,) * (len(shape) - 1 - position))
    return loudness


def bell_draw(rng, shape, spread, bound, shards=(), dtype=jnp.bfloat16):
    level = steps_of(rng, shape, shards, -0.22, 0.18) if shards else 1.0
    values = jax.random.normal(rng, shape, jnp.float32) * spread * level
    return jnp.minimum(jnp.maximum(values, -bound), bound).astype(dtype)


def setup_inputs(seed: int = 0) -> dict:
    splits = jax.random.split(jax.random.key(seed), 7)
    return {
        "acts": bell_draw(splits[0], (TOK, NQ, IN), 1.0, 6.0, ((0, 8), (2, 4))),
        "grads": bell_draw(splits[1], (TOK, NQ, OUT), 0.0625, 0.3984375, ((0, 4), (2, 8))),
        "basis_in": bell_draw(splits[2], (IN, IN), IN ** -0.5, 0.03125, ((0, 4), (1, 8))),
        "basis_out": bell_draw(splits[3], (OUT, OUT), OUT ** -0.5, 0.0625, ((0, 8), (1, 4))),
        "eigen": jnp.clip(jnp.exp(math.log(8.0) - 2.7725887 * jax.random.uniform(splits[4], (IN, OUT), jnp.float32) ** steps_of(splits[4], (IN, OUT), ((0, 8), (1, 4)), -0.2, 0.2)), 0.5, 8.0).astype(jnp.bfloat16),
        "sketch": bell_draw(splits[5], (SK, OUT), OUT ** -0.5, 0.0625, ((1, 8),)),
    }


def reference(acts, grads, basis_in, basis_out, eigen, sketch):
    act_rot = jnp.dot(acts.reshape(TOK * NQ, IN).astype(jnp.float32), basis_in.astype(jnp.float32), preferred_element_type=jnp.float32).astype(jnp.bfloat16).reshape(TOK, NQ, IN)
    grad_rot = jnp.dot(grads.reshape(TOK * NQ, OUT).astype(jnp.float32), basis_out.astype(jnp.float32), preferred_element_type=jnp.float32).astype(jnp.bfloat16).reshape(TOK, NQ, OUT)
    sketch_rot = jnp.dot(sketch.astype(jnp.float32), basis_out.astype(jnp.float32), preferred_element_type=jnp.float32).astype(jnp.bfloat16)
    eigen_wide = eigen.astype(jnp.float32)
    bases = []
    projections = []
    for query in range(NQ):
        core_sum = jnp.dot(act_rot[:, query, :].T.astype(jnp.float32), grad_rot[:, query, :].astype(jnp.float32), preferred_element_type=jnp.float32)
        scaled = (core_sum / eigen_wide).astype(jnp.bfloat16)
        reduced = jnp.dot(sketch_rot.astype(jnp.float32), scaled.T.astype(jnp.float32), preferred_element_type=jnp.float32).astype(jnp.bfloat16)
        range_rows = jnp.dot(reduced.astype(jnp.float32), basis_in.T.astype(jnp.float32), preferred_element_type=jnp.float32)
        gram = jnp.dot(range_rows, range_rows.T, precision=lax.Precision.HIGHEST)
        factor = jnp.linalg.cholesky(gram)
        basis_rows = lax.linalg.triangular_solve(factor, range_rows, left_side=True, lower=True)
        mapped = jnp.dot(basis_rows.astype(jnp.bfloat16).astype(jnp.float32), basis_in.astype(jnp.float32), preferred_element_type=jnp.float32).astype(jnp.bfloat16)
        core = jnp.dot(mapped.astype(jnp.float32), scaled.astype(jnp.float32), preferred_element_type=jnp.float32).astype(jnp.bfloat16)
        projection = jnp.dot(core.astype(jnp.float32), basis_out.T.astype(jnp.float32), preferred_element_type=jnp.float32)
        bases.append(basis_rows)
        projections.append(projection)
    return (jnp.stack(bases), jnp.stack(projections))
```

```python
import functools
import jax
import jax.numpy as jnp
from jax import lax
from jax.experimental import pallas as pl
from jax.experimental.pallas import tpu as pltpu
from jax.sharding import PartitionSpec as P

MESH = pl.DeviceIdType.MESH
VMEM = pl.BlockSpec(memory_space=pltpu.VMEM)
BAND = 16


def greet(axis, n, me):
    barrier = pltpu.get_barrier_semaphore()
    for k in range(1, n):
        pl.semaphore_signal(
            barrier, inc=1, device_id={axis: lax.rem(me + k, n)}, device_id_type=MESH
        )
    pl.semaphore_wait(barrier, n - 1)


def send(src, dst, sems, k, axis, peer):
    copy = pltpu.make_async_remote_copy(
        src_ref=src,
        dst_ref=dst,
        send_sem=sems[0].at[k - 1],
        recv_sem=sems[1].at[k - 1],
        device_id={axis: peer},
        device_id_type=MESH,
    )
    copy.start()
    return copy


def columns(ref, index, width):
    return ref.at[:, pl.ds(pl.multiple_of(index * width, width), width)]


def gather_kernel(axis, n, leading, x_ref, o_ref, send_sem, recv_sem, own_sem):
    me = lax.axis_index(axis)
    place = o_ref.at[me] if leading else columns(o_ref, me, x_ref.shape[1])
    greet(axis, n, me)
    copies = [
        send(x_ref, place, (send_sem, recv_sem), k, axis, lax.rem(me + k, n)) for k in range(1, n)
    ]
    own = pltpu.make_async_copy(x_ref, place, own_sem)
    own.start()
    own.wait()
    for copy in copies:
        copy.wait()


def add_slots(slots, n, out):
    def step(i, carry):
        rows = pl.ds(pl.multiple_of(i * BAND, BAND), BAND)
        total = slots[0, rows, :].astype(jnp.float32)
        for k in range(1, n):
            total = total + slots[k, rows, :].astype(jnp.float32)
        out[rows, :] = total.astype(out.dtype)
        return carry

    lax.fori_loop(0, slots.shape[1] // BAND, step, 0)


def fill_slots(axis, n, me, x_ref, slots, sems, own_sem):
    width = slots.shape[2]
    greet(axis, n, me)
    copies = []
    for k in range(1, n):
        peer = lax.rem(me + k, n)
        copies.append(send(columns(x_ref, peer, width), slots.at[k], sems, k, axis, peer))
    own = pltpu.make_async_copy(columns(x_ref, me, width), slots.at[0], own_sem)
    own.start()
    own.wait()
    for copy in copies:
        copy.wait()


def scatter_kernel(axis, n, x_ref, o_ref, slots, send_sem, recv_sem, own_sem):
    me = lax.axis_index(axis)
    fill_slots(axis, n, me, x_ref, slots, (send_sem, recv_sem), own_sem)
    add_slots(slots, n, o_ref)


def reduce_kernel(
    axis, n, x_ref, o_ref, slots, stage, send_sem, recv_sem, own_sem, send_two, recv_two, own_two
):
    me = lax.axis_index(axis)
    fill_slots(axis, n, me, x_ref, slots, (send_sem, recv_sem), own_sem)
    add_slots(slots, n, stage)
    place = columns(o_ref, me, slots.shape[2])
    copies = [
        send(stage, place, (send_two, recv_two), k, axis, lax.rem(me + k, n)) for k in range(1, n)
    ]
    own = pltpu.make_async_copy(stage, place, own_two)
    own.start()
    own.wait()
    for copy in copies:
        copy.wait()


def semaphores(n):
    return [
        pltpu.SemaphoreType.DMA((n - 1,)),
        pltpu.SemaphoreType.DMA((n - 1,)),
        pltpu.SemaphoreType.DMA,
    ]


def launch(kernel, name, number, shape, dtype, scratch, x):
    return pl.pallas_call(
        kernel,
        name=name,
        out_shape=jax.ShapeDtypeStruct(shape, dtype),
        in_specs=[VMEM],
        out_specs=VMEM,
        scratch_shapes=scratch,
        compiler_params=pltpu.CompilerParams(
            collective_id=number, has_side_effects=True, vmem_limit_bytes=40 * 2**20
        ),
    )(x)


def fits(x, width):
    return x.shape[0] % BAND == 0 and width % 128 == 0


def gather_rows(x, axis, n, number):
    if not fits(x, x.shape[1]):
        return lax.all_gather(x, axis, axis=0, tiled=True)
    kernel = functools.partial(gather_kernel, axis, n, True)
    full = launch(kernel, f"gather{number}", number, (n, *x.shape), x.dtype, semaphores(n), x)
    return full.reshape(n * x.shape[0], x.shape[1])


def gather_columns(x, axis, n, number):
    if not fits(x, x.shape[1]):
        return lax.all_gather(x, axis, axis=1, tiled=True)
    kernel = functools.partial(gather_kernel, axis, n, False)
    shape = (x.shape[0], n * x.shape[1])
    return launch(kernel, f"gather{number}", number, shape, x.dtype, semaphores(n), x)


def scatter_sum(x, axis, n, number):
    width = x.shape[1] // n
    if not fits(x, width):
        return lax.psum_scatter(x.astype(jnp.float32), axis, scatter_dimension=1, tiled=True)
    scratch = [pltpu.VMEM((n, x.shape[0], width), x.dtype), *semaphores(n)]
    kernel = functools.partial(scatter_kernel, axis, n)
    shape = (x.shape[0], width)
    return launch(kernel, f"scatter{number}", number, shape, jnp.float32, scratch, x)


def full_sum(x, axis, n, number):
    width = x.shape[1] // n
    if not fits(x, width):
        return lax.psum(x.astype(jnp.float32), axis).astype(jnp.bfloat16)
    scratch = [
        pltpu.VMEM((n, x.shape[0], width), x.dtype),
        pltpu.VMEM((x.shape[0], width), jnp.bfloat16),
        *semaphores(n),
        *semaphores(n),
    ]
    kernel = functools.partial(reduce_kernel, axis, n)
    return launch(kernel, f"sum{number}", number, x.shape, jnp.bfloat16, scratch, x)


def dot(a, b, contract):
    product = lax.dot_general(a, b, ((contract), ((), ())), preferred_element_type=jnp.float32)
    return product


def on_device(nrow, ncol, acts, grads, basis_in, basis_out, eigen, sketch):
    bf = jnp.bfloat16
    queries = acts.shape[1]
    flat = queries * sketch.shape[0]
    full_acts = gather_rows(acts.reshape(-1, acts.shape[2]), "col", ncol, 0)
    tokens = full_acts.shape[0] // queries
    act_rot = full_sum(dot(full_acts, basis_in, ((1,), (0,))).astype(bf), "row", nrow, 1)
    full_grads = gather_rows(grads.reshape(-1, grads.shape[2]), "row", nrow, 2)
    joined = jnp.concatenate([full_grads, sketch], axis=0)
    joined = jnp.pad(joined, ((0, -joined.shape[0] % BAND), (0, 0)))
    joined_sum = full_sum(dot(joined, basis_out, ((1,), (0,))).astype(bf), "col", ncol, 3)
    grad_rot = joined_sum[: tokens * queries].reshape(tokens, queries, -1)
    sketch_rot = joined_sum[tokens * queries : tokens * queries + sketch.shape[0]]
    core_sum = jnp.einsum(
        "tqj,tqp->qjp",
        act_rot.reshape(tokens, queries, -1),
        grad_rot,
        preferred_element_type=jnp.float32,
    )
    scaled = (core_sum / eigen.astype(jnp.float32)).astype(bf)
    reduced_part = jnp.einsum("qjp,sp->qsj", scaled, sketch_rot, preferred_element_type=jnp.float32)
    reduced = full_sum(reduced_part.astype(bf).reshape(flat, -1), "row", nrow, 4)
    range_part = dot(reduced, basis_in, ((1,), (1,))).astype(bf)
    range_rows = scatter_sum(range_part, "col", ncol, 5).reshape(queries, sketch.shape[0], -1)
    gram_piece = jnp.einsum("qsi,qri->qsr", range_rows, range_rows, precision=lax.Precision.HIGHEST)
    gram = lax.psum(gram_piece, ("row", "col"))
    factor = jnp.linalg.cholesky(gram)
    basis_piece = lax.linalg.triangular_solve(factor, range_rows, left_side=True, lower=True)
    basis_rows = gather_columns(basis_piece.astype(bf).reshape(flat, -1), "col", ncol, 6)
    mapped_part = dot(basis_rows, basis_in, ((1,), (0,))).astype(bf)
    mapped = full_sum(mapped_part, "row", nrow, 7).reshape(queries, sketch.shape[0], -1)
    core_part = jnp.einsum("qsj,qjp->qsp", mapped, scaled, preferred_element_type=jnp.float32)
    core = full_sum(core_part.astype(bf).reshape(flat, -1), "col", ncol, 8)
    projection_part = dot(core, basis_out, ((1,), (1,))).astype(bf)
    projected = full_sum(projection_part, "row", nrow, 9)
    shape = (queries, sketch.shape[0], -1)
    return (
        basis_rows.astype(jnp.float32).reshape(shape),
        projected.astype(jnp.float32).reshape(shape),
    )


def solution(mesh):
    in_specs = (
        P("col", None, "row"),
        P("row", None, "col"),
        P("row", "col"),
        P("col", "row"),
        P("col", "row"),
        P(None, "col"),
    )
    out_specs = (P(None, None, "row"), P(None, None, "col"))
    body = functools.partial(on_device, mesh.shape["row"], mesh.shape["col"])
    return jax.shard_map(body, mesh=mesh, in_specs=in_specs, out_specs=out_specs, check_vma=False)
```
